32 devices in a mesh: group: 4 (over x, core), dev: 8 (over z, y).
Axes of the slice: x: 2, y: 2, z: 4, core: 2. Of those that a mesh axis runs over, the one named last changes fastest.
Arguments:
- velocity: float32 [3, 256, 128, 128], P(None, ('group', 'dev')), may hold values from -3 to 3
- viscosity: float32 [256, 128, 128], P(('group', 'dev')), may hold values from 0.04 to 0.3
- sample_idx: int32 [32, 256], P(('group', 'dev')), may hold values from 0 to 255, as said below
- assign: int32 [32, 256], P(('group', 'dev')), may hold values from 0 to 8191, as said below
- params: float32 [3670016], P(('group', 'dev')), may hold values from -0.15 to 0.15
- adam_m: float32 [3670016], P(('group', 'dev')), may hold values from -0.3 to 0.3
- adam_v: float32 [3670016], P(('group', 'dev')), may hold values from 0.0001 to 0.01
Outputs:
- velocity_next: float32 [3, 256, 128, 128], P(None, ('group', 'dev'))
- prediction: float32 [8192, 1536], P(('group', 'dev'))
- new_params: float32 [3670016], P(('group', 'dev'))
- new_m: float32 [3670016], P(('group', 'dev'))
- new_v: float32 [3670016], P(('group', 'dev'))
The draws below stay inside these ranges and needn't reach their ends.
Inputs may be any that keep to these rules, and one draw needn't show every extreme that they name: `sample_idx`: each row holds 256 different patch numbers; 0 and the largest patch number appear in every row. `assign`: all entries together are a permutation of the 8192 learner slots; each row names exactly 8 slots of every block of 256 consecutive slots.
All inputs are finite; a program needn't handle non-finite values.
Results may differ from the reference program's by a relative error of at most 0.00011.
Values sent between devices are 32-bit elements; how exact they have to be, the bound alone decides.
No kernel may reach another device: no remote copies, remote signals or barrier semaphores. Data moves between devices by JAX's collectives and lax.ppermute only.
A program may use at most 192 MiB of HBM per device.

```python
import math
import jax
import jax.numpy as jnp
from jax import lax

PATCH = 8
D = 512
H = 2048
NY = 128
NZ = 128
TOK_DEV = 256
CX = 8
NX = 256
F = 1536
NPARAM = 3670016
TOKENS = 8192
N_GROUP = 4
N_DEV = 8


def draw_sample_idx(key, part):
    blocks = N_GROUP * N_DEV
    count = NY // PATCH * (NZ // PATCH)

    def one_row(row_key):
        pick_key, order_key = jax.random.split(row_key)
        middle = jax.random.permutation(pick_key, count - 2)[:TOK_DEV - 2].astype(jnp.int32) + 1
        row = jnp.concatenate([jnp.zeros((1,), jnp.int32), jnp.full((1,), count - 1, jnp.int32), middle])
        return jax.random.permutation(order_key, row).astype(jnp.int32)
    return jax.vmap(one_row)(jax.random.split(jax.random.fold_in(key, 11), blocks))


def draw_assign(key, part):
    blocks = N_GROUP * N_DEV
    per_peer = TOK_DEV // blocks
    base = jax.random.fold_in(key, 23)
    route_key, slot_key = jax.random.split(base)
    routes = jax.vmap(lambda k: jax.random.permutation(k, TOK_DEV))(jax.random.split(route_key, blocks)).astype(jnp.int32)
    places = jax.vmap(lambda k: jax.random.permutation(k, TOK_DEV))(jax.random.split(slot_key, blocks)).astype(jnp.int32)
    target = routes // per_peer
    within = routes % per_peer
    source = jnp.arange(blocks, dtype=jnp.int32)[:, None]
    return (target * TOK_DEV + places[target, source * per_peer + within]).astype(jnp.int32)


def shard_levels(rng, shape, pieces, smallest, top_value):
    def one(position, shards_of):
        draws = jax.random.uniform(jax.random.fold_in(jax.random.fold_in(rng, 6), position), (shards_of,), jnp.float32, smallest / len(pieces), top_value / len(pieces))
        return jnp.repeat(jnp.exp(draws), shape[position] // shards_of).reshape((-1,) + (1,) * (len(shape) - position - 1))

    loudness = one(*pieces[0])
    for cut in pieces[1:]:
        loudness = loudness * one(*cut)
    return loudness


def normal_values(rng, dims, width, reach, pieces=(), kind=jnp.bfloat16):
    values = width * jax.random.normal(rng, dims, jnp.float32)
    if pieces:
        values = values * shard_levels(rng, dims, pieces, -0.22, 0.18)
    return jnp.clip(values, -reach, reach).astype(kind)


def setup_inputs(seed: int = 0) -> dict:
    splits = jax.random.split(jax.random.key(seed), 8)
    velocity = normal_values(splits[0], (3, NX, NY, NZ), 0.5, 3.0, ((1, 32),), jnp.float32)
    viscosity = jnp.clip(jnp.exp(math.log(0.3) - 2.014903 * jax.random.uniform(splits[1], (NX, NY, NZ), jnp.float32) ** shard_levels(splits[1], (NX, NY, NZ), ((0, 32),), -0.2, 0.2)), 0.04, 0.3)
    sample_idx = draw_sample_idx(jax.random.fold_in(splits[7], 71), 0)
    assign = draw_assign(jax.random.fold_in(splits[7], 71), 0)
    params = normal_values(splits[4], (NPARAM,), 0.03, 0.15, ((0, 32),), jnp.float32)
    adam_m = normal_values(splits[5], (NPARAM,), 0.05, 0.3, ((0, 32),), jnp.float32)
    adam_v = jnp.clip(jnp.exp(math.log(0.01) - 4.6051702 * jax.random.uniform(splits[6], (NPARAM,), jnp.float32) ** shard_levels(splits[6], (NPARAM,), ((0, 32),), -0.2, 0.2)), 0.0001, 0.01)
    return {"velocity": velocity, "viscosity": viscosity, "sample_idx": sample_idx, "assign": assign, "params": params, "adam_m": adam_m, "adam_v": adam_v}


time_step = 0.5
norm_epsilon = 1e-06
beta_first = 0.9
beta_second = 0.95
learn_rate = 0.01
adam_epsilon = 1e-08
adam_count = 10

def advance(extended, visc_inner):
    centre = extended[:, 1:-1]
    upper_one = extended[:, 2:]
    lower_one = extended[:, :-2]
    upper_two = jnp.roll(centre, -1, 2)
    lower_two = jnp.roll(centre, 1, 2)
    upper_three = jnp.roll(centre, -1, 3)
    lower_three = jnp.roll(centre, 1, 3)
    laplace = upper_one + lower_one + upper_two + lower_two + upper_three + lower_three - 6.0 * centre
    advect = 0.5 * (centre[0:1] * (upper_one - lower_one) + centre[1:2] * (upper_two - lower_two) + centre[2:3] * (upper_three - lower_three))
    return centre + time_step * (visc_inner[None] * laplace - advect)

def patch_rows(block):
    depth = block.shape[1]
    span_y = block.shape[2] // depth
    span_z = block.shape[3] // depth
    tiles = block.reshape(3, depth, span_y, depth, span_z, depth).transpose(2, 4, 0, 1, 3, 5)
    return tiles.reshape(span_y * span_z, 3 * depth ** 3)

def matmul(left, right):
    return jnp.dot(left, right, precision=lax.Precision.HIGHEST, preferred_element_type=jnp.float32)

def forward(flat, inputs):
    first = F * D
    second = first + D * H
    third = second + H * D
    w_in = flat[:first].reshape(F, D)
    w_up = flat[first:second].reshape(D, H)
    w_down = flat[second:third].reshape(H, D)
    w_out = flat[third:].reshape(D, F)
    state = matmul(inputs, w_in)
    normed = state * lax.rsqrt(lax.optimization_barrier(jnp.mean(state * state, axis=-1, keepdims=True)) + norm_epsilon)
    hidden = jax.nn.gelu(matmul(normed, w_up), approximate=True)
    state = state + matmul(hidden, w_down)
    return inputs + matmul(state, w_out)

def batch_grad(flat, inputs, targets, count):

    def loss_fn(weights):
        guess = forward(weights, inputs)
        error = guess - targets
        return (0.5 * jnp.sum(error * error) / count, guess)
    loss, pull, guess = jax.vjp(loss_fn, flat, has_aux=True)
    grad, = pull(jnp.ones_like(loss))
    return (grad, guess)

def adam(shard, grad, moment, second):
    new_m = beta_first * moment + (1.0 - beta_first) * grad
    new_v = beta_second * second + (1.0 - beta_second) * grad * grad
    update = new_m / (1.0 - beta_first ** adam_count) / (jnp.sqrt(new_v / (1.0 - beta_second ** adam_count)) + adam_epsilon)
    return (shard - learn_rate * update, new_m, new_v)

def reference(velocity, viscosity, sample_idx, assign, params, adam_m, adam_v):
    blocks = N_GROUP * N_DEV
    padded_u = jnp.pad(velocity, ((0, 0), (2, 2), (0, 0), (0, 0)))
    padded_nu = jnp.pad(viscosity, ((2, 2), (0, 0), (0, 0)))

    def solve_block(item):
        index, rows = item
        start = index * CX
        extended = lax.dynamic_slice_in_dim(padded_u, start, CX + 4, 1)
        visc = lax.dynamic_slice_in_dim(padded_nu, start, CX + 4, 0)
        first = advance(extended, visc[1:-1])
        second = advance(first, visc[2:-2])
        current = first[:, 1:-1]
        return (second, patch_rows(current)[rows], patch_rows(second)[rows])
    stepped, tok_in, tok_out = lax.map(solve_block, (jnp.arange(blocks, dtype=jnp.int32), sample_idx))
    velocity_next = stepped.transpose(1, 0, 2, 3, 4).reshape(3, NX, NY, NZ)
    slots = assign.reshape(-1)
    inputs = jnp.zeros((TOKENS, F), jnp.float32).at[slots].set(tok_in.reshape(-1, F))
    targets = jnp.zeros((TOKENS, F), jnp.float32).at[slots].set(tok_out.reshape(-1, F))

    def learn(total, pair):
        grad, guess = batch_grad(params, pair[0], pair[1], TOK_DEV)
        return (total + grad, guess)
    grad, guesses = lax.scan(learn, jnp.zeros((NPARAM,), jnp.float32), (inputs.reshape(blocks, TOK_DEV, F), targets.reshape(blocks, TOK_DEV, F)))
    prediction = guesses.reshape(TOKENS, F)
    new_params, new_m, new_v = adam(params, grad, adam_m, adam_v)
    return (velocity_next, prediction, new_params, new_m, new_v)
```

```python
import functools

import jax
import jax.numpy as jnp
from jax import lax
from jax.experimental import pallas as pl
from jax.experimental.pallas import tpu as pltpu
from jax.sharding import PartitionSpec as P

time_step = 0.5
norm_epsilon = 1e-06
beta_first = 0.9
beta_second = 0.95
learn_rate = 0.01
adam_epsilon = 1e-08
adam_count = 10

AXES = ("group", "dev")
LANES = 128
GELU_A = 0.7978845608028654
GELU_B = 0.044715


def flat_ring(offset):
    count = lax.axis_size(AXES)
    if offset > 0:
        return [(i, i + 1) for i in range(count - 1)]
    return [(i + 1, i) for i in range(count - 1)]


def stepped(centre, upper, lower, nu):
    ny, nz = nu.shape
    out = []
    for c in range(3):
        mid = centre[c]
        up_y = pltpu.roll(mid, ny - 1, 0)
        lo_y = pltpu.roll(mid, 1, 0)
        up_z = pltpu.roll(mid, nz - 1, 1)
        lo_z = pltpu.roll(mid, 1, 1)
        laplace = upper[c] + lower[c] + up_y + lo_y + up_z + lo_z - 6.0 * mid
        advect = 0.5 * (
            centre[0] * (upper[c] - lower[c])
            + centre[1] * (up_y - lo_y)
            + centre[2] * (up_z - lo_z)
        )
        out.append(mid + time_step * (nu * laplace - advect))
    return out


def patch_columns(field_ref, out_ref, plane0, depth):
    ny, nz = field_ref.shape[2:]
    span = nz // depth
    per_tile = span // depth
    rows = (ny // depth) * span
    lane = lax.broadcasted_iota(jnp.int32, (1, 1, nz), 2) // depth
    row = lax.broadcasted_iota(jnp.int32, (1, span, 1), 1)

    def shear(block):
        bit = 1
        while bit < span:
            turned = pltpu.roll(block, bit * depth, 2)
            block = jnp.where((row & bit) != 0, turned, block)
            bit *= 2
        return block

    def one(t, carry):
        c = t // (depth // per_tile)
        dx = (t % (depth // per_tile)) * per_tile
        planes = [
            field_ref[c, plane0 + dx + k].reshape(ny // depth, depth, nz) for k in range(per_tile)
        ]
        block = jnp.concatenate(planes, axis=1)
        block = shear(block)
        bit = 1
        while bit < span:
            turned = pltpu.roll(block, span - bit, 1)
            block = jnp.where((lane & bit) != 0, turned, block)
            bit *= 2
        block = shear(block)
        out_ref[:, pl.ds(pl.multiple_of(t * LANES, LANES), LANES)] = block.reshape(rows, nz)
        return carry

    lax.fori_loop(0, 3 * depth // per_tile, one, 0)


def physics_kernel(vel, low, high, visc, next_out, in_out, target_out, wide, nu, first, second):
    depth = vel.shape[1]
    for c in range(3):
        wide[c, 0:2] = low[2 * c : 2 * c + 2]
        wide[c, 2 : 2 + depth] = vel[c]
        wide[c, 2 + depth : 4 + depth] = high[2 * c : 2 * c + 2]
    nu[0:1] = low[6:7]
    nu[1 : 1 + depth] = visc[...]
    nu[1 + depth : 2 + depth] = high[6:7]

    def step_one(i, carry):
        out = stepped(
            [wide[c, i + 1] for c in range(3)],
            [wide[c, i + 2] for c in range(3)],
            [wide[c, i] for c in range(3)],
            nu[i],
        )
        for c in range(3):
            first[c, i] = out[c]
        return carry

    lax.fori_loop(0, depth + 2, step_one, 0)

    def step_two(i, carry):
        out = stepped(
            [first[c, i + 1] for c in range(3)],
            [first[c, i + 2] for c in range(3)],
            [first[c, i] for c in range(3)],
            nu[i + 1],
        )
        for c in range(3):
            next_out[c, i] = out[c]
        return carry

    lax.fori_loop(0, depth, step_two, 0)
    patch_columns(first, in_out, 1, depth)
    patch_columns(next_out, target_out, 0, depth)


def physics(velocity, viscosity, low, high):
    _, depth, ny, nz = velocity.shape
    rows = (ny // depth) * (nz // depth)
    feats = 3 * depth**3
    f32 = jnp.float32
    vmem = pl.BlockSpec(memory_space=pltpu.VMEM)
    return pl.pallas_call(
        physics_kernel,
        name="physics",
        out_shape=(
            jax.ShapeDtypeStruct(velocity.shape, f32),
            jax.ShapeDtypeStruct((rows, feats), f32),
            jax.ShapeDtypeStruct((rows, feats), f32),
        ),
        in_specs=[vmem] * 4,
        out_specs=(vmem,) * 3,
        scratch_shapes=[
            pltpu.VMEM((3, depth + 4, ny, nz), f32),
            pltpu.VMEM((depth + 2, ny, nz), f32),
            pltpu.VMEM((3, depth + 2, ny, nz), f32),
            pltpu.VMEM((8, LANES), f32),
        ],
        compiler_params=pltpu.CompilerParams(vmem_limit_bytes=40 << 20),
        cost_estimate=pl.CostEstimate(
            flops=velocity.size * 120, bytes_accessed=velocity.size * 16, transcendentals=0
        ),
    )(velocity, low, high, viscosity)


NT = (((1,), (1,)), ((), ()))
TN = (((0,), (0,)), ((), ()))
NN = (((1,), (0,)), ((), ()))


def halves(value):
    top = value.astype(jnp.bfloat16)
    return top, (value - top.astype(jnp.float32)).astype(jnp.bfloat16)


def product(left, right, dims):
    dot = functools.partial(lax.dot_general, dimension_numbers=dims, preferred_element_type=jnp.float32)
    return dot(left[0], right[0]) + (dot(left[0], right[1]) + dot(left[1], right[0]))


def learn_kernel(
    shapes,
    count,
    flat_hbm,
    x_ref,
    t_ref,
    guess_out,
    grad_hbm,
    flat,
    in_hi, in_lo, up_hi, up_lo, down_hi, down_lo, out_hi, out_lo,
    pre,
    hid_hi, hid_lo,
    err_hi, err_lo,
    in_sems,
    out_sems,
):
    bases, total = [], 0
    for rows, cols in shapes:
        bases.append(total)
        total += rows * cols // LANES
    terms = [(in_hi, in_lo), (up_hi, up_lo), (down_hi, down_lo), (out_hi, out_lo)]

    def part(ref, k):
        rows, cols = shapes[k]
        return ref.at[pl.ds(bases[k], rows * cols // LANES)]

    loads = [
        pltpu.make_async_copy(part(flat_hbm, k), part(flat, k), in_sems.at[k]) for k in range(4)
    ]
    stores = [
        pltpu.make_async_copy(part(flat, k), part(grad_hbm, k), out_sems.at[k]) for k in range(4)
    ]
    for load in loads:
        load.start()

    def split(k):
        rows, cols = shapes[k]
        stride = cols // LANES
        hi, lo = terms[k]
        step = 128
        loads[k].wait()

        def some(i, carry):
            r = pl.multiple_of(i * step, step)
            for nb in range(stride):
                top, low = halves(flat[pl.ds(bases[k] + nb + r * stride, step, stride=stride), :])
                hi[pl.ds(r, step), nb * LANES : (nb + 1) * LANES] = top
                lo[pl.ds(r, step), nb * LANES : (nb + 1) * LANES] = low
            return carry

        lax.fori_loop(0, rows // step, some, 0)

    def weight(k, rows=slice(None), cols=slice(None)):
        return terms[k][0][rows, cols], terms[k][1][rows, cols]

    def keep_grad(k, row0, col0, value):
        _, cols = shapes[k]
        stride = cols // LANES
        rows, width = value.shape
        for nb in range(width // LANES):
            at = pl.ds(bases[k] + row0 * stride + col0 // LANES + nb, rows, stride=stride)
            flat[at, :] = value[:, nb * LANES : (nb + 1) * LANES]

    tokens, feats = x_ref.shape
    hidden = shapes[1][1]
    width = shapes[0][1]
    tile = 512

    split(0)
    state = product(halves(x_ref[...]), weight(0), NN)
    scale = lax.rsqrt(jnp.mean(state * state, axis=-1, keepdims=True) + norm_epsilon)
    normed = state * scale
    normed2 = halves(normed)
    split(1)
    for j in range(0, hidden, tile):
        cols = slice(j, j + tile)
        h = product(normed2, weight(1, cols=cols), NN)
        pre[:, cols] = h
        cdf = 0.5 * (1.0 + jnp.tanh(GELU_A * (h + GELU_B * (h * h * h))))
        hid_hi[:, cols], hid_lo[:, cols] = halves(h * cdf)
    split(2)
    state2 = state + product((hid_hi[...], hid_lo[...]), weight(2), NN)
    last = halves(state2)
    split(3)
    for j in range(0, feats, tile):
        cols = slice(j, j + tile)
        guess = x_ref[:, cols] + product(last, weight(3, cols=cols), NN)
        guess_out[:, cols] = guess
        error = (guess - t_ref[:, cols]) * (1.0 / count)
        err_hi[:, cols], err_lo[:, cols] = halves(error)

    for j in range(0, feats, tile):
        cols = slice(j, j + tile)
        keep_grad(3, 0, j, product(last, (err_hi[:, cols], err_lo[:, cols]), TN))
    stores[3].start()
    d_state = product((err_hi[...], err_lo[...]), weight(3), NT)
    d_last = halves(d_state)
    for j in range(0, hidden, tile):
        cols = slice(j, j + tile)
        keep_grad(2, j, 0, product((hid_hi[:, cols], hid_lo[:, cols]), d_last, TN))
        d_hid = product(d_last, weight(2, rows=cols), NT)
        h = pre[:, cols]
        tan = jnp.tanh(GELU_A * (h + GELU_B * (h * h * h)))
        slope = 0.5 * (1.0 + tan) + 0.5 * h * (1.0 - tan * tan) * (
            GELU_A * (1.0 + 3.0 * GELU_B * (h * h))
        )
        d_pre = halves(d_hid * slope)
        keep_grad(1, 0, j, product(normed2, d_pre, TN))
        hid_hi[:, cols], hid_lo[:, cols] = d_pre
    stores[2].start()
    stores[1].start()
    d_normed = product((hid_hi[...], hid_lo[...]), weight(1), NT)
    inner = jnp.mean(d_normed * normed, axis=-1, keepdims=True)
    d_state = d_state + scale * (d_normed - normed * inner)
    d_first = halves(d_state)
    for j in range(0, feats, tile):
        cols = slice(j, j + tile)
        keep_grad(0, j, 0, product(halves(x_ref[:, cols]), d_first, TN))
    stores[0].start()
    for store in stores:
        store.wait()


def learn(flat, inputs, targets, shapes, count):
    f32, bf16 = jnp.float32, jnp.bfloat16
    tokens, feats = inputs.shape
    hidden = shapes[1][1]
    vmem = pl.BlockSpec(memory_space=pltpu.VMEM)
    hbm = pl.BlockSpec(memory_space=pl.ANY)
    scratch = [pltpu.VMEM(flat.shape, f32)]
    for shape in shapes:
        scratch += [pltpu.VMEM(shape, bf16)] * 2
    scratch += [pltpu.VMEM((tokens, hidden), f32)]
    scratch += [pltpu.VMEM((tokens, hidden), bf16)] * 2
    scratch += [pltpu.VMEM((tokens, feats), bf16)] * 2
    scratch += [pltpu.SemaphoreType.DMA((4,)), pltpu.SemaphoreType.DMA((4,))]
    return pl.pallas_call(
        functools.partial(learn_kernel, shapes, count),
        name="learn",
        out_shape=(
            jax.ShapeDtypeStruct((tokens, feats), f32),
            jax.ShapeDtypeStruct(flat.shape, f32),
        ),
        in_specs=[hbm, vmem, vmem],
        out_specs=(vmem, hbm),
        scratch_shapes=scratch,
        compiler_params=pltpu.CompilerParams(vmem_limit_bytes=62 << 20),
        cost_estimate=pl.CostEstimate(
            flops=tokens * flat.size * 18, bytes_accessed=flat.size * 8, transcendentals=tokens * hidden * 2
        ),
    )(flat, inputs, targets)


def adam(shard, grad, moment, second):
    new_m = beta_first * moment + (1.0 - beta_first) * grad
    new_v = beta_second * second + (1.0 - beta_second) * grad * grad
    update = (
        new_m
        / (1.0 - beta_first**adam_count)
        / (jnp.sqrt(new_v / (1.0 - beta_second**adam_count)) + adam_epsilon)
    )
    return (shard - learn_rate * update, new_m, new_v)


def gather_params(params):
    return lax.all_gather(params.reshape(-1, LANES), AXES, axis=0, tiled=True)


def scatter_grad(grad):
    return lax.psum_scatter(grad.reshape(-1), AXES, scatter_dimension=0, tiled=True)


def local(shapes, velocity, viscosity, sample_idx, assign, params, adam_m, adam_v):
    flat = gather_params(params)
    _, depth, ny, nz = velocity.shape
    planes = lambda a, b: jnp.concatenate(
        [velocity[:, a : a + 2].reshape(6, ny, nz), viscosity[b : b + 1]], 0
    )
    low = lax.ppermute(planes(depth - 2, depth - 1), AXES, flat_ring(1))
    high = lax.ppermute(planes(0, 0), AXES, flat_ring(-1))

    slots = assign.shape[1]
    owner = assign[0] // slots
    order = jnp.argsort(owner, stable=True)
    span = nz // depth
    patch = sample_idx[0][order]
    rows = patch - patch % span + (span - patch % span) % span
    place = lax.all_to_all(
        (assign[0][order] % slots)[:, None], AXES, split_axis=0, concat_axis=0, tiled=True
    )[:, 0]
    source = jnp.zeros((slots,), jnp.int32).at[place].set(jnp.arange(slots, dtype=jnp.int32))

    velocity_next, inputs, targets = physics(velocity, viscosity, low, high)
    guess, grad = learn(flat, inputs, targets, shapes, slots)
    got = lax.all_to_all(guess[rows], AXES, split_axis=0, concat_axis=0, tiled=True)
    prediction = got[source]
    new_params, new_m, new_v = adam(params, scatter_grad(grad), adam_m, adam_v)
    return (velocity_next, prediction, new_params, new_m, new_v)


def solution(mesh):
    block = P(AXES)
    slab = P(None, AXES, None, None)

    def step(velocity, viscosity, sample_idx, assign, params, adam_m, adam_v):
        devices = mesh.size
        depth = velocity.shape[1] // devices
        feats = 3 * depth**3
        wide = 512
        hidden = (params.size - 2 * feats * wide) // (2 * wide)
        assert 2 * wide * (feats + hidden) == params.size
        assert sample_idx.shape[1] * depth**2 == velocity.shape[2] * velocity.shape[3]
        shapes = ((feats, wide), (wide, hidden), (hidden, wide), (wide, feats))
        return jax.shard_map(
            functools.partial(local, shapes),
            mesh=mesh,
            in_specs=(slab, block, block, block, block, block, block),
            out_specs=(slab, block, block, block, block),
            check_vma=False,
        )(velocity, viscosity, sample_idx, assign, params, adam_m, adam_v)

    return step
```

```python
import functools
import itertools

import jax
import jax.numpy as jnp
import numpy as np
from jax import lax
from jax.experimental import pallas as pl
from jax.experimental.pallas import tpu as pltpu
from jax.sharding import PartitionSpec as P

time_step = 0.5
norm_epsilon = 1e-06
beta_first = 0.9
beta_second = 0.95
learn_rate = 0.01
adam_epsilon = 1e-08
adam_count = 10

AXES = ("group", "dev")
LANES = 128
GELU_A = 0.7978845608028654
GELU_B = 0.044715


def flat_ring(offset):
    count = lax.axis_size(AXES)
    if offset > 0:
        return [(i, i + 1) for i in range(count - 1)]
    return [(i + 1, i) for i in range(count - 1)]


def stepped(centre, upper, lower, nu):
    ny, nz = nu.shape
    out = []
    for c in range(3):
        mid = centre[c]
        up_y = pltpu.roll(mid, ny - 1, 0)
        lo_y = pltpu.roll(mid, 1, 0)
        up_z = pltpu.roll(mid, nz - 1, 1)
        lo_z = pltpu.roll(mid, 1, 1)
        laplace = upper[c] + lower[c] + up_y + lo_y + up_z + lo_z - 6.0 * mid
        advect = 0.5 * (
            centre[0] * (upper[c] - lower[c])
            + centre[1] * (up_y - lo_y)
            + centre[2] * (up_z - lo_z)
        )
        out.append(mid + time_step * (nu * laplace - advect))
    return out


def patch_columns(field_ref, out_ref, plane0, depth):
    ny, nz = field_ref.shape[2:]
    span = nz // depth
    per_tile = span // depth
    rows = (ny // depth) * span
    lane = lax.broadcasted_iota(jnp.int32, (1, 1, nz), 2) // depth
    row = lax.broadcasted_iota(jnp.int32, (1, span, 1), 1)

    def shear(block):
        bit = 1
        while bit < span:
            turned = pltpu.roll(block, bit * depth, 2)
            block = jnp.where((row & bit) != 0, turned, block)
            bit *= 2
        return block

    def one(t, carry):
        c = t // (depth // per_tile)
        dx = (t % (depth // per_tile)) * per_tile
        planes = [
            field_ref[c, plane0 + dx + k].reshape(ny // depth, depth, nz) for k in range(per_tile)
        ]
        block = jnp.concatenate(planes, axis=1)
        block = shear(block)
        bit = 1
        while bit < span:
            turned = pltpu.roll(block, span - bit, 1)
            block = jnp.where((lane & bit) != 0, turned, block)
            bit *= 2
        block = shear(block)
        out_ref[:, pl.ds(pl.multiple_of(t * LANES, LANES), LANES)] = block.reshape(rows, nz)
        return carry

    lax.fori_loop(0, 3 * depth // per_tile, one, 0)


def physics_kernel(vel, low, high, visc, next_out, in_out, target_out, wide, nu, first, second):
    depth = vel.shape[1]
    for c in range(3):
        wide[c, 0:2] = low[2 * c : 2 * c + 2]
        wide[c, 2 : 2 + depth] = vel[c]
        wide[c, 2 + depth : 4 + depth] = high[2 * c : 2 * c + 2]
    nu[0:1] = low[6:7]
    nu[1 : 1 + depth] = visc[...]
    nu[1 + depth : 2 + depth] = high[6:7]

    def step_one(i, carry):
        out = stepped(
            [wide[c, i + 1] for c in range(3)],
            [wide[c, i + 2] for c in range(3)],
            [wide[c, i] for c in range(3)],
            nu[i],
        )
        for c in range(3):
            first[c, i] = out[c]
        return carry

    lax.fori_loop(0, depth + 2, step_one, 0)

    def step_two(i, carry):
        out = stepped(
            [first[c, i + 1] for c in range(3)],
            [first[c, i + 2] for c in range(3)],
            [first[c, i] for c in range(3)],
            nu[i + 1],
        )
        for c in range(3):
            next_out[c, i] = out[c]
        return carry

    lax.fori_loop(0, depth, step_two, 0)
    patch_columns(first, in_out, 1, depth)
    patch_columns(next_out, target_out, 0, depth)


def physics(velocity, viscosity, low, high):
    _, depth, ny, nz = velocity.shape
    rows = (ny // depth) * (nz // depth)
    feats = 3 * depth**3
    f32 = jnp.float32
    vmem = pl.BlockSpec(memory_space=pltpu.VMEM)
    return pl.pallas_call(
        physics_kernel,
        name="physics",
        out_shape=(
            jax.ShapeDtypeStruct(velocity.shape, f32),
            jax.ShapeDtypeStruct((rows, feats), f32),
            jax.ShapeDtypeStruct((rows, feats), f32),
        ),
        in_specs=[vmem] * 4,
        out_specs=(vmem,) * 3,
        scratch_shapes=[
            pltpu.VMEM((3, depth + 4, ny, nz), f32),
            pltpu.VMEM((depth + 2, ny, nz), f32),
            pltpu.VMEM((3, depth + 2, ny, nz), f32),
            pltpu.VMEM((8, LANES), f32),
        ],
        compiler_params=pltpu.CompilerParams(vmem_limit_bytes=40 << 20),
        cost_estimate=pl.CostEstimate(
            flops=velocity.size * 120, bytes_accessed=velocity.size * 16, transcendentals=0
        ),
    )(velocity, low, high, viscosity)


NT = (((1,), (1,)), ((), ()))
TN = (((0,), (0,)), ((), ()))
NN = (((1,), (0,)), ((), ()))


def halves(value):
    top = value.astype(jnp.bfloat16)
    return top, (value - top.astype(jnp.float32)).astype(jnp.bfloat16)


def product(left, right, dims):
    dot = functools.partial(lax.dot_general, dimension_numbers=dims, preferred_element_type=jnp.float32)
    return dot(left[0], right[0]) + (dot(left[0], right[1]) + dot(left[1], right[0]))


def learn_kernel(
    shapes,
    count,
    n_in,
    n_out,
    rows_in,
    rows_out,
    x_ref,
    t_ref,
    *refs,
):
    pieces_in, refs = refs[:n_in], refs[n_in:]
    guess_out, refs = refs[0], refs[1:]
    pieces_out, refs = refs[:n_out], refs[n_out:]
    learn_body(shapes, count, rows_in, rows_out, x_ref, t_ref, pieces_in, guess_out, pieces_out, *refs)


def learn_body(
    shapes,
    count,
    rows_in,
    rows_out,
    x_ref,
    t_ref,
    pieces_in,
    guess_out,
    pieces_out,
    flat,
    in_hi, in_lo, up_hi, up_lo, down_hi, down_lo, out_hi, out_lo,
    pre,
    hid_hi, hid_lo,
    err_hi, err_lo,
    in_sems,
    out_sems,
):
    bases, total = [], 0
    for rows, cols in shapes:
        bases.append(total)
        total += rows * cols // LANES
    terms = [(in_hi, in_lo), (up_hi, up_lo), (down_hi, down_lo), (out_hi, out_lo)]

    def at_rows(table, i, rows):
        return flat.at[pl.ds(pl.multiple_of(table[i], 8), rows)]

    loads, stores = [], []
    for ref in pieces_in:
        for b in range(ref.shape[0]):
            i = len(loads)
            loads.append(
                pltpu.make_async_copy(ref.at[b], at_rows(rows_in, i, ref.shape[1]), in_sems.at[i])
            )
    for ref in pieces_out:
        for b in range(ref.shape[0]):
            i = len(stores)
            stores.append(
                pltpu.make_async_copy(at_rows(rows_out, i, ref.shape[1]), ref.at[b], out_sems.at[i])
            )
    for load in loads:
        load.start()
    for load in loads:
        load.wait()

    def split(k):
        rows, cols = shapes[k]
        stride = cols // LANES
        hi, lo = terms[k]
        step = 128

        def some(i, carry):
            r = pl.multiple_of(i * step, step)
            for nb in range(stride):
                top, low = halves(flat[pl.ds(bases[k] + nb + r * stride, step, stride=stride), :])
                hi[pl.ds(r, step), nb * LANES : (nb + 1) * LANES] = top
                lo[pl.ds(r, step), nb * LANES : (nb + 1) * LANES] = low
            return carry

        lax.fori_loop(0, rows // step, some, 0)

    def weight(k, rows=slice(None), cols=slice(None)):
        return terms[k][0][rows, cols], terms[k][1][rows, cols]

    def keep_grad(k, row0, col0, value):
        _, cols = shapes[k]
        stride = cols // LANES
        rows, width = value.shape
        for nb in range(width // LANES):
            at = pl.ds(bases[k] + row0 * stride + col0 // LANES + nb, rows, stride=stride)
            flat[at, :] = value[:, nb * LANES : (nb + 1) * LANES]

    tokens, feats = x_ref.shape
    hidden = shapes[1][1]
    width = shapes[0][1]
    tile = 512

    split(0)
    state = product(halves(x_ref[...]), weight(0), NN)
    scale = lax.rsqrt(jnp.mean(state * state, axis=-1, keepdims=True) + norm_epsilon)
    normed = state * scale
    normed2 = halves(normed)
    split(1)
    for j in range(0, hidden, tile):
        cols = slice(j, j + tile)
        h = product(normed2, weight(1, cols=cols), NN)
        pre[:, cols] = h
        cdf = 0.5 * (1.0 + jnp.tanh(GELU_A * (h + GELU_B * (h * h * h))))
        hid_hi[:, cols], hid_lo[:, cols] = halves(h * cdf)
    split(2)
    state2 = state + product((hid_hi[...], hid_lo[...]), weight(2), NN)
    last = halves(state2)
    split(3)
    for j in range(0, feats, tile):
        cols = slice(j, j + tile)
        guess = x_ref[:, cols] + product(last, weight(3, cols=cols), NN)
        guess_out[:, cols] = guess
        error = (guess - t_ref[:, cols]) * (1.0 / count)
        err_hi[:, cols], err_lo[:, cols] = halves(error)

    for j in range(0, feats, tile):
        cols = slice(j, j + tile)
        keep_grad(3, 0, j, product(last, (err_hi[:, cols], err_lo[:, cols]), TN))
    d_state = product((err_hi[...], err_lo[...]), weight(3), NT)
    d_last = halves(d_state)
    for j in range(0, hidden, tile):
        cols = slice(j, j + tile)
        keep_grad(2, j, 0, product((hid_hi[:, cols], hid_lo[:, cols]), d_last, TN))
        d_hid = product(d_last, weight(2, rows=cols), NT)
        h = pre[:, cols]
        tan = jnp.tanh(GELU_A * (h + GELU_B * (h * h * h)))
        slope = 0.5 * (1.0 + tan) + 0.5 * h * (1.0 - tan * tan) * (
            GELU_A * (1.0 + 3.0 * GELU_B * (h * h))
        )
        d_pre = halves(d_hid * slope)
        keep_grad(1, 0, j, product(normed2, d_pre, TN))
        hid_hi[:, cols], hid_lo[:, cols] = d_pre
    d_normed = product((hid_hi[...], hid_lo[...]), weight(1), NT)
    inner = jnp.mean(d_normed * normed, axis=-1, keepdims=True)
    d_state = d_state + scale * (d_normed - normed * inner)
    d_first = halves(d_state)
    for j in range(0, feats, tile):
        cols = slice(j, j + tile)
        keep_grad(0, j, 0, product(halves(x_ref[:, cols]), d_first, TN))
    for store in stores:
        store.start()
    for store in stores:
        store.wait()


def learn(pieces, rows_in, out_shapes, rows_out, inputs, targets, shapes, count):
    f32, bf16 = jnp.float32, jnp.bfloat16
    tokens, feats = inputs.shape
    hidden = shapes[1][1]
    total = sum(rows * cols for rows, cols in shapes)
    vmem = pl.BlockSpec(memory_space=pltpu.VMEM)
    smem = pl.BlockSpec(memory_space=pltpu.SMEM)
    hbm = pl.BlockSpec(memory_space=pl.ANY)
    scratch = [pltpu.VMEM((total // LANES, LANES), f32)]
    for shape in shapes:
        scratch += [pltpu.VMEM(shape, bf16)] * 2
    scratch += [pltpu.VMEM((tokens, hidden), f32)]
    scratch += [pltpu.VMEM((tokens, hidden), bf16)] * 2
    scratch += [pltpu.VMEM((tokens, feats), bf16)] * 2
    scratch += [pltpu.SemaphoreType.DMA(rows_in.shape), pltpu.SemaphoreType.DMA(rows_out.shape)]
    guess, *grads = pl.pallas_call(
        functools.partial(learn_kernel, shapes, count, len(pieces), len(out_shapes)),
        name="learn",
        out_shape=(jax.ShapeDtypeStruct((tokens, feats), f32),)
        + tuple(jax.ShapeDtypeStruct(shape, f32) for shape in out_shapes),
        in_specs=[smem, smem, vmem, vmem] + [hbm] * len(pieces),
        out_specs=(vmem,) + (hbm,) * len(out_shapes),
        scratch_shapes=scratch,
        compiler_params=pltpu.CompilerParams(vmem_limit_bytes=62 << 20),
        cost_estimate=pl.CostEstimate(
            flops=tokens * total * 18, bytes_accessed=total * 8, transcendentals=tokens * hidden * 2
        ),
    )(rows_in, rows_out, inputs, targets, *pieces)
    return guess, grads


def adam(shard, grad, moment, second):
    new_m = beta_first * moment + (1.0 - beta_first) * grad
    new_v = beta_second * second + (1.0 - beta_second) * grad * grad
    update = (
        new_m
        / (1.0 - beta_first**adam_count)
        / (jnp.sqrt(new_v / (1.0 - beta_second**adam_count)) + adam_epsilon)
    )
    return (shard - learn_rate * update, new_m, new_v)


def moved(value, axes, move):
    sizes = (2, 2, 4, 2)
    pairs = []
    for here in itertools.product(*(range(n) for n in sizes)):
        there = move(*here)
        if there is not None:
            pairs.append(tuple(functools.reduce(lambda a, b: a * b[0] + b[1], zip(sizes, p), 0) for p in (here, there)))
    return lax.ppermute(value, axes, pairs)


def core(x, c, z, y):
    return (x, 1 - c, z, y)


def near(x, c, z, y):
    return (x, c, z, 1 - y) if c == 0 else (1 - x, c, z, y)


def far(x, c, z, y):
    return (1 - x, c, z, y) if c == 0 else (x, c, z, 1 - y)


def pair(x, c, z, y):
    return (x, c, z ^ 1, y)


def middle(x, c, z, y):
    return (x, c, 3 - z, y) if z in (1, 2) else None


def outward(x, c, z, y):
    return (x, c, 0 if z == 1 else 3, y) if z in (1, 2) else None


def inward(x, c, z, y):
    return (x, c, 1 if z == 0 else 2, y) if z in (0, 3) else None


def place(axes):
    g, d = lax.axis_index(axes[0]), lax.axis_index(axes[1])
    return g // 2, g % 2, d // 2, d % 2


def block_rows(axes, rows, half, order, dp, dq, owner):
    x, _, z, y = place(axes)
    step_x, step_y = (dp, dq) if half == 0 else (dq, dp)
    low = z < 2
    far_z = (z, z ^ 1, jnp.where(low, 2, 1), jnp.where(low, 3, 0))[order]
    shard = (((x ^ step_x) * 2 + owner) * 4 + far_z) * 2 + (y ^ step_y)
    return shard * rows + half * (rows // 2)


def piece_rows(axes, rows, order, mine, dp, dq):
    c = lax.axis_index(axes[0]) % 2
    at = [block_rows(axes, rows, half, order, dp, dq, owner) for half in (0, 1) for owner in (0, 1)]
    first = (c == 0) == mine
    return [jnp.where(first, at[o], at[2 + o]) for o in (0, 1)]


def gather_pieces(params, axes):
    shard = params.reshape(-1, LANES)
    rows = shard.shape[0]
    c = lax.axis_index(axes[0]) % 2
    parts = shard.reshape(2, rows // 2, LANES)
    mine = lax.dynamic_index_in_dim(parts, c, 0, False)
    got = moved(lax.dynamic_index_in_dim(parts, 1 - c, 0, False), axes, core)
    own = jnp.where(c == 0, jnp.stack([mine, got]), jnp.stack([got, mine]))
    one = moved(own, axes, pair)
    two_mid = moved(own, axes, middle)
    two_end = moved(two_mid, axes, outward)
    three_mid = moved(one, axes, middle)
    three_end = moved(three_mid, axes, outward)
    pieces, table = [], []
    for order, block in enumerate((own, one, two_mid + two_end, three_mid + three_end)):
        q = moved(block, axes, near)
        p = moved(block, axes, far)
        both = moved(q, axes, far)
        for value, dp, dq in ((block, 0, 0), (q, 0, 1), (p, 1, 0), (both, 1, 1)):
            pieces += [value, moved(value, axes, core)]
            table += piece_rows(axes, rows, order, True, dp, dq)
            table += piece_rows(axes, rows, order, False, dp, dq)
    return pieces, jnp.stack(table)


def scatter_rows(rows, axes):
    table = []
    for mine in (True, False):
        for order in (3, 2, 1, 0):
            for dp, dq in ((1, 1), (1, 0), (0, 1), (0, 0)):
                table += piece_rows(axes, rows, order, mine, dp, dq)
    return [(8, rows // 2, LANES)] * 8, jnp.stack(table)


def scatter_pieces(grads, axes):
    grads = [g.reshape(4, 2, g.shape[1], LANES) for g in grads]
    parts = []
    for mine, other in zip(grads[:4], grads[4:]):
        got = moved(other, axes, core)
        p = moved(mine[0:2] + got[0:2], axes, far)
        q = moved((mine[2] + got[2]) + p[0], axes, near)
        parts.append((mine[3] + got[3]) + p[1] + q)
    three = moved(parts[0], axes, inward)
    three = moved(parts[0] + three, axes, middle)
    two = moved(parts[1], axes, inward)
    two = moved(parts[1] + two, axes, middle)
    one = moved(parts[2] + three, axes, pair)
    total = parts[3] + one + two
    c = lax.axis_index(axes[0]) % 2
    keep = lax.dynamic_index_in_dim(total, c, 0, False)
    got = moved(lax.dynamic_index_in_dim(total, 1 - c, 0, False), axes, core)
    return jnp.where(c == 0, jnp.concatenate([keep, got]), jnp.concatenate([got, keep])).reshape(-1)


def gather_flat(params, axes):
    flat = lax.all_gather(params.reshape(-1, LANES), axes, axis=0, tiled=True)
    return [flat[None]], jnp.zeros((1,), jnp.int32)


def flat_rows(rows, axes):
    return [(1, rows * lax.axis_size(axes), LANES)], jnp.zeros((1,), jnp.int32)


def scatter_flat(grads, axes):
    return lax.psum_scatter(grads[0].reshape(-1), axes, scatter_dimension=0, tiled=True)


def local(shapes, exchange, velocity, viscosity, sample_idx, assign, params, adam_m, adam_v):
    gather, result_rows, scatter = exchange
    pieces, rows_in = gather(params, AXES)
    out_shapes, rows_out = result_rows(params.size // LANES, AXES)
    _, depth, ny, nz = velocity.shape
    planes = lambda a, b: jnp.concatenate(
        [velocity[:, a : a + 2].reshape(6, ny, nz), viscosity[b : b + 1]], 0
    )
    low = lax.ppermute(planes(depth - 2, depth - 1), AXES, flat_ring(1))
    high = lax.ppermute(planes(0, 0), AXES, flat_ring(-1))

    slots = assign.shape[1]
    owner = assign[0] // slots
    order = jnp.argsort(owner, stable=True)
    span = nz // depth
    patch = sample_idx[0][order]
    rows = patch - patch % span + (span - patch % span) % span
    slot = lax.all_to_all(
        (assign[0][order] % slots)[:, None], AXES, split_axis=0, concat_axis=0, tiled=True
    )[:, 0]
    source = jnp.zeros((slots,), jnp.int32).at[slot].set(jnp.arange(slots, dtype=jnp.int32))

    velocity_next, inputs, targets = physics(velocity, viscosity, low, high)
    guess, grads = learn(pieces, rows_in, out_shapes, rows_out, inputs, targets, shapes, slots)
    got = lax.all_to_all(guess[rows], AXES, split_axis=0, concat_axis=0, tiled=True)
    prediction = got[source]
    new_params, new_m, new_v = adam(params, scatter(grads, AXES), adam_m, adam_v)
    return (velocity_next, prediction, new_params, new_m, new_v)


def chip_lines(mesh):
    if tuple(mesh.devices.shape) != (4, 8):
        return False
    return all(
        tuple(d.coords) == (g // 2, i % 2, i // 2) and d.core_on_chip == g % 2
        for (g, i), d in np.ndenumerate(mesh.devices)
    )


def solution(mesh):
    block = P(AXES)
    if chip_lines(mesh):
        exchange = (gather_pieces, scatter_rows, scatter_pieces)
    else:
        exchange = (gather_flat, flat_rows, scatter_flat)
    slab = P(None, AXES, None, None)

    def step(velocity, viscosity, sample_idx, assign, params, adam_m, adam_v):
        devices = mesh.size
        depth = velocity.shape[1] // devices
        feats = 3 * depth**3
        wide = 512
        hidden = (params.size - 2 * feats * wide) // (2 * wide)
        assert 2 * wide * (feats + hidden) == params.size
        assert sample_idx.shape[1] * depth**2 == velocity.shape[2] * velocity.shape[3]
        shapes = ((feats, wide), (wide, hidden), (hidden, wide), (wide, feats))
        return jax.shard_map(
            functools.partial(local, shapes, exchange),
            mesh=mesh,
            in_specs=(slab, block, block, block, block, block, block),
            out_specs=(slab, block, block, block, block),
            check_vma=False,
        )(velocity, viscosity, sample_idx, assign, params, adam_m, adam_v)

    return step
```
